32 devices in a mesh: section: 2 (over core), expert: 16 (over z, y, x).
Axes of the slice: x: 2, y: 2, z: 4, core: 2. Of those that a mesh axis runs over, the one named last changes fastest.
Arguments:
- fwd_states: bfloat16 [2, 2048, 2048], P('section', 'expert'), may hold values from -16 to 16
- fwd_routes: int32 [2, 2048, 2], P('section', 'expert'), may hold values from 0 to 15, all different within a row; in each aligned block of 128 rows (0 to 127, 128 to 255, ..., all dimensions but the last counted through in order) at most 20 rows name the same one
- bwd_states: bfloat16 [2, 2048, 2048], P('section', 'expert'), may hold values from -16 to 16
- bwd_routes: int32 [2, 2048, 2], P('section', 'expert'), may hold values from 0 to 15, all different within a row; in each aligned block of 128 rows (0 to 127, 128 to 255, ..., all dimensions but the last counted through in order) at most 20 rows name the same one
- bwd_cot: bfloat16 [2, 2048, 2048], P('section', 'expert'), may hold values from -1.5 to 1.5
- w_in: bfloat16 [16, 512, 2048], P('expert', 'section'), may hold values from -0.125 to 0.125
- w_out: bfloat16 [16, 512, 2048], P('expert', 'section'), may hold values from -0.25 to 0.25
Outputs:
- next_states: bfloat16 [2, 2048, 2048], P('section', 'expert')
- prev_cot: bfloat16 [2, 2048, 2048], P('section', 'expert')
- grad_w_in: float32 [16, 512, 2048], P('expert', 'section')
- grad_w_out: float32 [16, 512, 2048], P('expert', 'section')
The draws below stay inside these ranges and needn't reach their ends.
Inputs may be any that keep to these rules, and one draw needn't show every extreme that they name: `fwd_routes`: each row names 2 different experts; in each aligned block of 128 rows (the rows of one device in one section) no expert is named by more than 20 rows, and in some block one expert is named by exactly 20 rows. `bwd_routes`: each row names 2 different experts; in each aligned block of 128 rows (the rows of one device in one section) no expert is named by more than 20 rows, and in some block one expert is named by exactly 20 rows.
All inputs are finite; a program needn't handle non-finite values.
Results may differ from the reference program's by a relative error of at most 0.012.
Values may be sent and summed in bfloat16 or wider, within the bound.
A program may use at most 64 MiB of HBM per device.

```python
import math
import jax
import jax.numpy as jnp
import numpy as np
from jax import lax

D = 2048
H = 512
K = 2
TOK_DEV = 128
EXPERTS = 16
SECTIONS = 2
TOKENS = 2048
CAP = 20
N_EXPERT = 16


def draw_states(key, salt):
    key = jax.random.fold_in(key, salt)
    keys = jax.random.split(key, 3)
    full_shape = (SECTIONS, TOKENS, D)
    base = jax.random.normal(keys[0], full_shape, jnp.float32)
    row_scale = jnp.exp(jax.random.uniform(keys[1], (SECTIONS, TOKENS, 1), jnp.float32, math.log(0.3), math.log(3.0)))
    col_scale = jnp.exp(jax.random.uniform(keys[2], (1, 1, D), jnp.float32, math.log(0.3), math.log(3.0)))
    return jnp.clip(base * row_scale * col_scale, -16.0, 16.0).astype(jnp.bfloat16)


def draw_fwd_states(key, part):
    return draw_states(key, 11)


def draw_bwd_states(key, part):
    return draw_states(key, 23)


def shard_levels(own_key, dims, pieces, low, top_value):
    gain = 1.0
    for dim, parts in pieces:
        draws = jax.random.uniform(jax.random.fold_in(jax.random.fold_in(own_key, 6), dim), (parts,), jnp.float32, low / len(pieces), top_value / len(pieces))
        gain = gain * jnp.repeat(jnp.exp(draws), dims[dim] // parts).reshape((-1,) + (1,) * (len(dims) - 1 - dim))
    return gain


def deal_out(stream_key, own, number, rows, count, top, reach, slope):
    sequence = jax.random.permutation(stream_key, count)
    crowded, usual = portions_of(count, rows * top, reach, slope, True), portions_of(count, rows * top, reach, slope, False)
    places = jnp.arange(count)

    def named(sizes, turn):
        used = int((sizes > 0).sum())
        fixed = max(1, used // 4)
        passed = fixed + (places - fixed + turn * (used - fixed)) % max(1, count - fixed)
        return jnp.zeros((count,), jnp.int32).at[sequence[jnp.where(places < fixed, places, passed)]].set(jnp.asarray(sizes, jnp.int32))

    sizes = jnp.where(number % 4 == 0, named(crowded, number // 4), named(usual, number - number // 4 - 1))
    mixed = jax.random.permutation(jax.random.fold_in(own, 3), count)
    giver, taker = mixed[0:count // 2 * 2:2], mixed[1:count // 2 * 2:2]
    margin = jnp.minimum(sizes[giver] - 1, reach - sizes[taker]) // 2
    margin = jnp.where((giver == sequence[0]) | (taker == sequence[0]) | (sizes[taker] == 0), 0, jnp.maximum(margin, 0))
    passed = jax.random.randint(jax.random.fold_in(own, 4), (count // 2,), 0, 1 << 20) % (margin + 1)
    sizes = sizes.at[giver].add(-passed).at[taker].add(passed)
    members = jnp.searchsorted(jnp.cumsum(sizes), jnp.arange(rows * top), side="right").astype(jnp.int32)
    table = members.reshape(top, rows).T
    table = table[jax.random.permutation(jax.random.fold_in(own, 1), rows)]
    turn = jax.random.randint(jax.random.fold_in(own, 2), (rows, 1), 0, top)
    return jnp.take_along_axis(table, (jnp.arange(top)[None, :] + turn) % top, axis=1)


def portions_of(count, total, limit, lean, full):
    weights = [(1 << 20) // math.isqrt(standing ** lean) + 1 for standing in range(1, count + 1)]
    largest = limit if full else min(limit, max(-(-total // count), total * weights[0] // sum(weights)))
    least = 1 if total - largest >= count - 1 else 0
    holding, rest = [largest] + [least] * (count - 1), total - largest - least * (count - 1)
    while rest > 0:
        free = [i for i in range(1, count) if holding[i] < largest] or [i for i in range(1, count) if holding[i] < limit]
        pool, budget = sum([weights[i] for i in free]), rest
        for i in free:
            more = min(limit - holding[i], max(1, budget * weights[i] // pool), rest)
            holding[i] = holding[i] + more
            rest = rest - more
    return np.array(holding)


def scatter_about(stream_key, dims, scale, bound, cuts=(), kind=jnp.bfloat16):
    drawn = scale * jax.random.normal(stream_key, dims, jnp.float32)
    if cuts:
        drawn = drawn * shard_levels(stream_key, dims, cuts, -0.22, 0.18)
    return jnp.clip(drawn, -bound, bound).astype(kind)


def setup_inputs(seed: int = 0) -> dict:
    key_of = jax.random.split(jax.random.key(seed), 8)
    fwd_states = draw_fwd_states(jax.random.fold_in(key_of[7], 71), 0)
    fwd_routes_keys = jax.random.split(jax.random.fold_in(key_of[1], 1), SECTIONS * TOKENS // TOK_DEV)
    fwd_routes_turns = jax.random.permutation(jax.random.fold_in(key_of[1], 3), SECTIONS * TOKENS // TOK_DEV)
    fwd_routes = jax.vmap(lambda own, number: deal_out(jax.random.fold_in(key_of[1], 2), own, number, TOK_DEV, EXPERTS, K, CAP, 2))(fwd_routes_keys, fwd_routes_turns).reshape((SECTIONS, TOKENS, K))
    bwd_states = draw_bwd_states(jax.random.fold_in(key_of[7], 71), 0)
    bwd_routes_keys = jax.random.split(jax.random.fold_in(key_of[3], 1), SECTIONS * TOKENS // TOK_DEV)
    bwd_routes_turns = jax.random.permutation(jax.random.fold_in(key_of[3], 3), SECTIONS * TOKENS // TOK_DEV)
    bwd_routes = jax.vmap(lambda own, number: deal_out(jax.random.fold_in(key_of[3], 2), own, number, TOK_DEV, EXPERTS, K, CAP, 2))(bwd_routes_keys, bwd_routes_turns).reshape((SECTIONS, TOKENS, K))
    bwd_cot = scatter_about(key_of[4], (SECTIONS, TOKENS, D), 0.25, 1.5, ((0, 2), (1, 16)))
    w_in = scatter_about(key_of[5], (EXPERTS, H, D), D ** -0.5, 0.125, ((0, 16), (1, 2)))
    w_out = scatter_about(key_of[6], (EXPERTS, H, D), H ** -0.5, 0.25, ((0, 16), (1, 2)))
    return {"fwd_states": fwd_states, "fwd_routes": fwd_routes, "bwd_states": bwd_states, "bwd_routes": bwd_routes, "bwd_cot": bwd_cot, "w_in": w_in, "w_out": w_out}


EPSILON = 1e-06

def norm_rows(states):
    x_wide = states.astype(jnp.float32)
    inv_rms = lax.rsqrt(lax.optimization_barrier(jnp.mean(x_wide * x_wide, axis=-1, keepdims=True)) + EPSILON)
    return (x_wide, inv_rms, (x_wide * inv_rms).astype(jnp.bfloat16))

def contract_last(first_op, second_op):
    return lax.dot_general(first_op, second_op, (((1,), (1,)), ((), ())), preferred_element_type=jnp.float32)

def silu_slope(pre_act):
    sigma = jax.nn.sigmoid(pre_act)
    return sigma * (1.0 + pre_act * (1.0 - sigma))

def expert_table(expert_ids):
    flat_ids = expert_ids.reshape(-1).astype(jnp.int32)
    entries = flat_ids.shape[0]
    sorted_order = jnp.argsort(flat_ids, stable=True).astype(jnp.int32)
    ranked = flat_ids[sorted_order]
    starts = jnp.searchsorted(ranked, jnp.arange(EXPERTS, dtype=jnp.int32), side='left').astype(jnp.int32)
    rank_pos = jnp.arange(entries, dtype=jnp.int32) - starts[ranked]
    expert_depth = N_EXPERT * CAP
    row_table = jnp.full((EXPERTS * expert_depth,), entries, dtype=jnp.int32)
    row_table = row_table.at[ranked * expert_depth + rank_pos].set(sorted_order)
    return row_table.reshape(EXPERTS, expert_depth)

def spread_rows(values, top_count):
    zero_row = jnp.zeros((1, values.shape[-1]), values.dtype)
    return jnp.concatenate([jnp.repeat(values, top_count, axis=0), zero_row], axis=0)

def place_back(expert_outs, row_table, entries, top_count):
    placed = jnp.zeros((entries + 1, D), jnp.bfloat16).at[row_table.reshape(-1)].set(expert_outs.reshape(-1, D))
    picked = placed[:entries].reshape(-1, top_count, D).astype(jnp.float32)
    return lax.optimization_barrier(jnp.sum(picked, axis=1))

def forward_section(states, expert_ids, w_in, w_out):
    x_wide, inv_rms, normed = norm_rows(states)
    row_table = expert_table(expert_ids)
    top_count = expert_ids.shape[-1]
    spread = spread_rows(normed, top_count)

    def one_expert(operands):
        row_index, weight_in, weight_out = operands
        row_block = spread[row_index]
        hidden = jax.nn.silu(contract_last(row_block, weight_in)).astype(jnp.bfloat16)
        return jnp.dot(hidden, weight_out, preferred_element_type=jnp.float32).astype(jnp.bfloat16)
    expert_outs = lax.map(one_expert, (row_table, w_in, w_out))
    summed = place_back(expert_outs, row_table, spread.shape[0] - 1, top_count)
    return (x_wide + summed).astype(jnp.bfloat16)

def backward_section(states, expert_ids, cot, w_in, w_out):
    x_wide, inv_rms, normed = norm_rows(states)
    row_table = expert_table(expert_ids)
    top_count = expert_ids.shape[-1]
    spread_u = spread_rows(normed, top_count)
    spread_g = spread_rows(cot, top_count)

    def one_expert(operands):
        row_index, weight_in, weight_out = operands
        rows_u = spread_u[row_index]
        rows_g = spread_g[row_index]
        pre_act = contract_last(rows_u, weight_in)
        hidden = jax.nn.silu(pre_act).astype(jnp.bfloat16)
        grad_h = (contract_last(rows_g, weight_out) * silu_slope(pre_act)).astype(jnp.bfloat16)
        grad_u = jnp.dot(grad_h, weight_in, preferred_element_type=jnp.float32).astype(jnp.bfloat16)
        term_in = jnp.dot(grad_h.T, rows_u, preferred_element_type=jnp.float32).astype(jnp.bfloat16)
        term_out = jnp.dot(hidden.T, rows_g, preferred_element_type=jnp.float32).astype(jnp.bfloat16)
        return (grad_u, term_in, term_out)
    grad_u, term_in, term_out = lax.map(one_expert, (row_table, w_in, w_out))
    summed = place_back(grad_u, row_table, spread_u.shape[0] - 1, top_count)
    cot_wide = cot.astype(jnp.float32)
    cubed = inv_rms * inv_rms * inv_rms
    grad_x = cot_wide + inv_rms * summed - x_wide * cubed * lax.optimization_barrier(jnp.mean(summed * x_wide, axis=-1, keepdims=True))
    return (grad_x.astype(jnp.bfloat16), term_in, term_out)

def reference(fwd_states, fwd_routes, bwd_states, bwd_routes, bwd_cot, w_in, w_out):

    def forward_one(operands):
        return forward_section(operands[0], operands[1], w_in, w_out)
    outputs = lax.map(forward_one, (fwd_states, fwd_routes))

    def backward_one(totals, operands):
        grad_x, term_in, term_out = backward_section(operands[0], operands[1], operands[2], w_in, w_out)
        return ((totals[0] + term_in.astype(jnp.float32), totals[1] + term_out.astype(jnp.float32)), grad_x)
    empty_grad = jnp.zeros(w_in.shape, jnp.float32)
    (grad_in, grad_out), grads_x = lax.scan(backward_one, (empty_grad, empty_grad), (bwd_states, bwd_routes, bwd_cot))
    return (jnp.roll(outputs, 1, axis=0), jnp.roll(grads_x, -1, axis=0), grad_in, grad_out)
```

```python
import functools
import jax
import jax.numpy as jnp
from jax import lax
from jax.experimental import pallas as pl
from jax.experimental.pallas import tpu as pltpu
from jax.sharding import PartitionSpec as P

EPSILON = 1e-06
GROUPS = 4
F32, BF16 = jnp.float32, jnp.bfloat16
NT = (((1,), (1,)), ((), ()))
NN = (((1,), (0,)), ((), ()))
TN = (((0,), (0,)), ((), ()))


def mm(a, b, dims):
    return lax.dot_general(a, b, dims, preferred_element_type=F32)


def kernel(
    experts, sections, cap,
    xf_ref, rf_ref, xb_ref, rb_ref, g_ref, win_ref, wout_ref,
    next_ref, prev_ref, gin_ref, gout_ref,
    send, home, recv, w_in, w_out, u_tok, far_tok, far_routes, u_rows, g_rows, act, slope, hid, tails, part_in, part_out,
    pm, pt, spread, summed, result,
    a2a_send, a2a_recv, tok_send, tok_recv, route_send, route_recv, relay_send, w_send, w_recv, p_send, p_recv, s_send, s_recv,
):
    q = GROUPS
    tokens, depth = xf_ref.shape
    width = depth // q
    main = cap // 16 * 16
    tail = cap - main
    own_h = win_ref.shape[0]
    n_main = experts * main
    me = lax.axis_index("expert")
    sec = lax.axis_index("section")
    near = experts // 2
    quarter = experts // 4
    half = me // near
    place = lax.rem(me, near)
    layer = me // quarter
    column = lax.rem(me, quarter)
    client = lax.rem(layer, 2)
    my_relay = (2 - half) * quarter + column
    relaying = jnp.logical_or(layer == 1, layer == 2)

    def cols(j):
        return pl.ds(pl.multiple_of(j * width, width), width)

    barrier = pltpu.get_barrier_semaphore()

    @pl.loop(1, experts)
    def _(k):
        pl.semaphore_signal(barrier, inc=1, device_id={"expert": lax.rem(me + k, experts)})

    @pl.loop(1, sections)
    def _(k):
        pl.semaphore_signal(barrier, inc=1, device_id={"section": lax.rem(sec + k, sections)})

    own_rows = pl.ds(pl.multiple_of(sec * own_h, own_h), own_h)
    for i, (src, dst) in enumerate(((win_ref, w_in), (wout_ref, w_out))):
        pltpu.make_async_copy(src, dst.at[own_rows], w_recv.at[i]).start()

    def routing(which, routes):
        lane_e = lax.broadcasted_iota(jnp.int32, (tokens, experts), 1)
        eye = (
            lax.broadcasted_iota(jnp.int32, (tokens, tokens), 0)
            == lax.broadcasted_iota(jnp.int32, (tokens, tokens), 1)
        ).astype(F32)
        columns = mm(eye.astype(BF16), routes.astype(F32).astype(BF16), NT)
        wide = [columns[:, k : k + 1] for k in range(routes.shape[0])]
        hits = [(i == lane_e.astype(F32)).astype(F32) for i in wide]
        table = functools.reduce(jnp.add, hits)
        later = (
            lax.broadcasted_iota(jnp.int32, (tokens, tokens), 0)
            > lax.broadcasted_iota(jnp.int32, (tokens, tokens), 1)
        ).astype(F32)
        rank = mm(later.astype(BF16), table.astype(BF16), NN)
        pos = [jnp.sum(h * rank, axis=1, keepdims=True) for h in hits]
        if main:
            lane = lax.broadcasted_iota(jnp.int32, (tokens, n_main), 1).astype(F32)
            hit = jnp.zeros((tokens, n_main), F32)
            for i, p in zip(wide, pos):
                hit = jnp.where(lane == jnp.where(p < main, i * main + p, -1.0), 1.0, hit)
            pm[which] = hit.astype(BF16)
        if tail:
            n_tail = experts * q * tail
            lane = lax.broadcasted_iota(jnp.int32, (tokens, n_tail), 1).astype(F32)
            for j in range(q):
                hit = jnp.zeros((tokens, n_tail), F32)
                for i, p in zip(wide, pos):
                    slot = jnp.where(p >= main, i * (q * tail) + (p - main) + j * tail, -1.0)
                    hit = jnp.where(lane == slot, 1.0, hit)
                pt[which, j] = hit.astype(BF16)

    def normalize(x_ref, which):
        @pl.loop(0, tokens // 16)
        def _(i):
            rows = pl.ds(pl.multiple_of(i * 16, 16), 16)
            x = x_ref[rows, :].astype(F32)
            inv = lax.rsqrt(jnp.mean(x * x, axis=-1, keepdims=True) + EPSILON)
            u_tok[which, rows, :] = (x * inv).astype(BF16)

    def dispatch(which, src, slot, group):
        chunks = pl.ds(group * near, near)
        if tail:
            tails[: near * q * tail, :] = jnp.zeros((near * q * tail, width), F32)

        @pl.loop(0, q)
        def _(j):
            piece = src[:, cols(j)]
            if main:
                lanes = pl.ds(pl.multiple_of(half * (near * main), near * main), near * main)
                send[slot, chunks, pl.ds(pl.multiple_of(j * main, main), main), :] = (
                    mm(pm[which, :, lanes], piece, TN).astype(BF16).reshape(near, main, width)
                )
            if tail:
                size = near * q * tail
                lanes = pl.ds(pl.multiple_of(half * size, size), size)
                tails[:size, :] += mm(pt[which, j, :, lanes], piece, TN)

        if tail:
            send[slot, chunks, q * main :, :] = (
                tails[: near * q * tail, :].astype(BF16).reshape(near, q * tail, width)
            )

    def to_near(slot, group, source, sem):
        pltpu.make_async_copy(
            send.at[slot, group * near + place], recv.at[slot, source], a2a_recv.at[slot]
        ).start()

        @pl.loop(1, near)
        def _(k):
            spot = lax.rem(place + k, near)
            pltpu.make_async_remote_copy(
                src_ref=send.at[slot, group * near + spot],
                dst_ref=recv.at[slot, source],
                send_sem=sem,
                recv_sem=a2a_recv.at[slot],
                device_id={"expert": half * near + spot},
            ).start()

    def to_relay(slot, src):
        pltpu.make_async_remote_copy(
            src_ref=src, dst_ref=far_tok.at[slot, client],
            send_sem=tok_send.at[slot], recv_sem=tok_recv.at[slot, client],
            device_id={"expert": my_relay},
        ).start()

    def routes_to_relay(micro, src):
        pltpu.make_async_remote_copy(
            src_ref=src, dst_ref=far_routes.at[micro, client],
            send_sem=route_send.at[micro], recv_sem=route_recv.at[micro, client],
            device_id={"expert": my_relay},
        ).start()

    def relay(slot):
        micro = min(slot, 1)

        @pl.when(relaying)
        def _():
            @pl.loop(0, 2)
            def _(c):
                which = 2 + c
                if slot < 2:
                    mine = far_routes.at[micro, c]
                    pltpu.make_async_copy(mine, mine, route_recv.at[micro, c]).wait()
                    routing(which, far_routes[micro, c])
                block = far_tok.at[slot, c]
                pltpu.make_async_copy(block, block, tok_recv.at[slot, c]).wait()
                dispatch(which, block, slot, 1 + c)
                source = (1 - half) * near + c * quarter + column
                to_near(slot, 1 + c, source, relay_send.at[slot])

    def exchange(slot):
        pltpu.make_async_copy(home.at[slot - 3, me], recv.at[slot, me], a2a_recv.at[slot]).start()

        @pl.loop(1, experts)
        def _(k):
            peer = lax.rem(me + k, experts)
            pltpu.make_async_remote_copy(
                src_ref=home.at[slot - 3, peer],
                dst_ref=recv.at[slot, me],
                send_sem=a2a_send.at[slot],
                recv_sem=a2a_recv.at[slot],
                device_id={"expert": peer},
            ).start()

    def arrived(slot):
        pltpu.make_async_copy(recv.at[slot], recv.at[slot], a2a_recv.at[slot]).wait()

    def unpack(slot, rows_ref):
        buf = recv.at[slot]

        @pl.loop(0, q)
        def _(j):
            if main:
                rows_ref[:n_main, cols(j)] = buf[
                    :, pl.ds(pl.multiple_of(j * main, main), main), :
                ].reshape(n_main, width)
            if tail:
                for b in range(2):
                    packed = buf[b * near : (b + 1) * near, q * main :, :]
                    rows_ref[n_main + b * near * tail : n_main + (b + 1) * near * tail, cols(j)] = mm(
                        spread[j], packed.reshape(near * q * tail, width), NN
                    ).astype(BF16)

    def contract(rows_ref, weight, total):
        total[...] = jnp.zeros_like(total)

        @pl.loop(0, q)
        def _(j):
            total[...] += mm(rows_ref[:, cols(j)], weight[:, cols(j)], NT)

    def expand(weight, slot):
        buf = home.at[slot - 3]
        if tail:
            tails[...] = jnp.zeros_like(tails)

        @pl.loop(0, q)
        def _(j):
            out = mm(hid[...], weight[:, cols(j)], NN).astype(BF16)
            if main:
                buf[:, pl.ds(pl.multiple_of(j * main, main), main), :] = out[:n_main].reshape(
                    experts, main, width
                )
            if tail:
                for b in range(2):
                    block = out[n_main + b * near * tail : n_main + (b + 1) * near * tail]
                    packed = slice(b * near * q * tail, (b + 1) * near * q * tail)
                    tails[packed, :] += mm(spread[j], block, TN)

        if tail:
            buf[:, q * main :, :] = tails[...].astype(BF16).reshape(experts, q * tail, width)

    def combine(which, slot):
        buf = recv.at[slot]

        @pl.loop(0, q)
        def _(j):
            total = jnp.zeros((tokens, width), F32)
            if main:
                block = buf[:, pl.ds(pl.multiple_of(j * main, main), main), :]
                total += mm(pm[which], block.reshape(n_main, width), NN)
            if tail:
                packed = buf[:, q * main :, :].reshape(experts * q * tail, width)
                total += mm(pt[which, j], packed, NN)
            summed[:, cols(j)] = total

    def weight_terms(left, right, part):
        @pl.loop(0, q)
        def _(j):
            part[:, cols(j)] = mm(left, right[:, cols(j)], TN).astype(BF16)

    normalize(xf_ref, 0)
    pl.semaphore_wait(barrier, experts + sections - 2)
    to_relay(0, u_tok.at[0])
    routes_to_relay(0, rf_ref)
    routes_to_relay(1, rb_ref)
    routing(0, rf_ref[...])
    dispatch(0, u_tok.at[0], 0, 0)
    to_near(0, 0, me, a2a_send.at[0])
    for i, (src, dst) in enumerate(((win_ref, w_in), (wout_ref, w_out))):
        @pl.loop(1, sections)
        def _(k):
            pltpu.make_async_remote_copy(
                src_ref=src, dst_ref=dst.at[own_rows],
                send_sem=w_send.at[i], recv_sem=w_recv.at[i],
                device_id={"section": lax.rem(sec + k, sections)},
            ).start()

    normalize(xb_ref, 1)
    to_relay(1, u_tok.at[1])
    to_relay(2, g_ref)
    routing(1, rb_ref[...])
    dispatch(1, u_tok.at[1], 1, 0)
    to_near(1, 0, me, a2a_send.at[1])
    dispatch(1, g_ref, 2, 0)
    to_near(2, 0, me, a2a_send.at[2])

    if tail:
        shape = (near * tail, near * q * tail)
        row = lax.broadcasted_iota(jnp.int32, shape, 0).astype(F32)
        col = lax.broadcasted_iota(jnp.int32, shape, 1).astype(F32)
        start = row + jnp.floor((row + 0.5) * (1.0 / tail)) * ((q - 1) * tail)
        for j in range(q):
            spread[j] = jnp.where(col == start + j * tail, 1.0, 0.0).astype(BF16)

    for i, dst in enumerate((w_in, w_out)):
        pltpu.make_async_copy(dst, dst, w_recv.at[i]).wait()

    relay(0)
    arrived(0)
    unpack(0, u_rows)
    contract(u_rows, w_in, act)
    hid[...] = jax.nn.silu(act[...]).astype(BF16)
    expand(w_out, 3)
    exchange(3)

    relay(1)
    relay(2)
    arrived(1)
    unpack(1, u_rows)
    contract(u_rows, w_in, act)
    arrived(2)
    unpack(2, g_rows)
    contract(g_rows, w_out, slope)
    sigma = jax.nn.sigmoid(act[...])
    hid[...] = (slope[...] * (sigma * (1.0 + act[...] * (1.0 - sigma)))).astype(BF16)
    expand(w_in, 4)
    exchange(4)
    weight_terms(hid[...], u_rows, part_in)
    hid[...] = jax.nn.silu(act[...]).astype(BF16)
    weight_terms(hid[...], g_rows, part_out)
    for i, (part, out) in enumerate(((part_in, gin_ref), (part_out, gout_ref))):
        pltpu.make_async_copy(part.at[own_rows], out.at[sec], p_recv.at[i]).start()

        @pl.loop(1, sections)
        def _(k):
            peer = lax.rem(sec + k, sections)
            pltpu.make_async_remote_copy(
                src_ref=part.at[pl.ds(pl.multiple_of(peer * own_h, own_h), own_h)],
                dst_ref=out.at[sec],
                send_sem=p_send.at[i], recv_sem=p_recv.at[i],
                device_id={"section": peer},
            ).start()

    arrived(3)
    combine(0, 3)

    @pl.loop(0, tokens // 16)
    def _(i):
        rows = pl.ds(pl.multiple_of(i * 16, 16), 16)
        result[0, rows, :] = (xf_ref[rows, :].astype(F32) + summed[rows, :]).astype(BF16)

    to_next = pltpu.make_async_remote_copy(
        src_ref=result.at[0], dst_ref=next_ref, send_sem=s_send.at[0], recv_sem=s_recv.at[0],
        device_id={"section": lax.rem(sec + 1, sections)},
    )
    to_next.start()

    arrived(4)
    combine(1, 4)

    @pl.loop(0, tokens // 16)
    def _(i):
        rows = pl.ds(pl.multiple_of(i * 16, 16), 16)
        x = xb_ref[rows, :].astype(F32)
        total = summed[rows, :]
        inv = lax.rsqrt(jnp.mean(x * x, axis=-1, keepdims=True) + EPSILON)
        proj = jnp.mean(total * x, axis=-1, keepdims=True)
        grad = g_ref[rows, :].astype(F32) + inv * total - x * (inv * inv * inv) * proj
        result[1, rows, :] = grad.astype(BF16)

    to_prev = pltpu.make_async_remote_copy(
        src_ref=result.at[1], dst_ref=prev_ref, send_sem=s_send.at[1], recv_sem=s_recv.at[1],
        device_id={"section": lax.rem(sec + sections - 1, sections)},
    )
    to_prev.start()

    for i, (src, out) in enumerate(((win_ref, gin_ref), (wout_ref, gout_ref))):
        pltpu.make_async_copy(out, out, p_recv.at[i]).wait()

        @pl.loop(1, sections)
        def _(k):
            pltpu.make_async_copy(src, src, w_send.at[i]).wait()
            pltpu.make_async_copy(src, src, p_send.at[i]).wait()

    fewer = send.at[0, pl.ds(0, near - 1)]
    for slot in range(3):
        pltpu.make_async_copy(fewer, fewer, a2a_send.at[slot]).wait()
        pltpu.make_async_copy(g_ref, g_ref, tok_send.at[slot]).wait()

        @pl.when(relaying)
        def _():
            for _ in range(2):
                pltpu.make_async_copy(fewer, fewer, relay_send.at[slot]).wait()

    for micro, src in enumerate((rf_ref, rb_ref)):
        pltpu.make_async_copy(src, src, route_send.at[micro]).wait()
    others = home.at[0, pl.ds(0, experts - 1)]
    for slot in (3, 4):
        pltpu.make_async_copy(others, others, a2a_send.at[slot]).wait()
    to_next.wait()
    to_prev.wait()


def per_device(fwd_states, fwd_routes, bwd_states, bwd_routes, bwd_cot, w_in, w_out):
    experts, sections = lax.axis_size("expert"), lax.axis_size("section")
    _, tokens, depth = fwd_states.shape
    top = fwd_routes.shape[2]
    own_h = w_in.shape[1]
    full_h = own_h * sections
    q = GROUPS
    cap = max(2, (5 * tokens * top + 4 * experts - 1) // (4 * experts))
    cap = -(-cap // 4) * 4
    main = cap // 16 * 16
    tail = cap - main
    rows = experts * cap
    width = depth // q
    n_tail = max(16, experts * q * tail)
    grant = (46 if experts * cap <= 512 and full_h * experts <= 8192 else 62) * 1000 * 1024
    vmem = pl.BlockSpec(memory_space=pltpu.VMEM)
    anywhere = pl.BlockSpec(memory_space=pl.ANY)
    sems = pltpu.SemaphoreType.DMA
    states = jax.ShapeDtypeStruct((tokens, depth), BF16)
    parts = jax.ShapeDtypeStruct((sections, own_h, depth), BF16)
    next_states, prev_cot, part_in, part_out = pl.pallas_call(
        functools.partial(kernel, experts, sections, cap),
        out_shape=(states, states, parts, parts),
        in_specs=[vmem] * 5 + [anywhere] * 2,
        out_specs=(anywhere,) * 4,
        scratch_shapes=[
            pltpu.VMEM((3, experts // 2 * 3, q * cap, width), BF16),
            pltpu.VMEM((2, experts, q * cap, width), BF16),
            pltpu.VMEM((5, experts, q * cap, width), BF16),
            pltpu.VMEM((full_h, depth), BF16),
            pltpu.VMEM((full_h, depth), BF16),
            pltpu.VMEM((2, tokens, depth), BF16),
            pltpu.VMEM((3, 2, tokens, depth), BF16),
            pltpu.VMEM((2, 2, top, tokens), jnp.int32),
            pltpu.VMEM((rows, depth), BF16),
            pltpu.VMEM((rows, depth), BF16),
            pltpu.VMEM((rows, full_h), F32),
            pltpu.VMEM((rows, full_h), F32),
            pltpu.VMEM((rows, full_h), BF16),
            pltpu.VMEM((n_tail, width), F32),
            pltpu.VMEM((full_h, depth), BF16),
            pltpu.VMEM((full_h, depth), BF16),
            pltpu.VMEM((4, tokens, max(16, experts * main)), BF16),
            pltpu.VMEM((4, q, tokens, n_tail), BF16),
            pltpu.VMEM((q, max(16, experts // 2 * tail), max(16, experts // 2 * q * tail)), BF16),
            pltpu.VMEM((tokens, depth), F32),
            pltpu.VMEM((2, tokens, depth), BF16),
            sems((5,)), sems((5,)), sems((3,)), sems((3, 2)), sems((2,)), sems((2, 2)), sems((3,)),
            sems((2,)), sems((2,)),
            sems((2,)), sems((2,)), sems((2,)), sems((2,)),
        ],
        compiler_params=pltpu.CompilerParams(
            collective_id=0, has_side_effects=True, vmem_limit_bytes=grant
        ),
    )(fwd_states[0], fwd_routes[0].T, bwd_states[0], bwd_routes[0].T, bwd_cot[0], w_in[0], w_out[0])
    grad_in = jnp.sum(part_in.astype(F32), axis=0)
    grad_out = jnp.sum(part_out.astype(F32), axis=0)
    return next_states[None], prev_cot[None], grad_in[None], grad_out[None]


def solution(mesh):
    in_specs = (P("section", "expert", None),) * 5 + (P("expert", "section", None),) * 2
    out_specs = (P("section", "expert", None),) * 2 + (P("expert", "section", None),) * 2
    return jax.shard_map(
        per_device, mesh=mesh, in_specs=in_specs, out_specs=out_specs, check_vma=False
    )
```

```python
import functools
import jax
import jax.numpy as jnp
from jax import lax
from jax.experimental import pallas as pl
from jax.experimental.pallas import tpu as pltpu
from jax.sharding import PartitionSpec as P

EPSILON = 1e-06
GROUPS = 4
F32, BF16 = jnp.float32, jnp.bfloat16
NT = (((1,), (1,)), ((), ()))
NN = (((1,), (0,)), ((), ()))
TN = (((0,), (0,)), ((), ()))


def mm(a, b, dims):
    return lax.dot_general(a, b, dims, preferred_element_type=F32)


def kernel(
    experts, sections, cap,
    xf_hbm, rf_hbm, xb_hbm, rb_hbm, g_hbm, win_ref, wout_ref,
    next_ref, prev_ref, gin_ref, gout_ref,
    xf_ref, rf_ref, xb_ref, rb_ref, g_ref,
    send, home, recv, w_in, w_out, u_tok, far_tok, far_routes, u_rows, g_rows, act, slope, hid, tails, part_in, part_out,
    pm, pt, spread, summed, result,
    loaded, a2a_send, a2a_recv, tok_send, tok_recv, route_send, route_recv, relay_send, w_send, w_recv, p_send, p_recv, s_send, s_recv,
):
    q = GROUPS
    tokens, depth = xf_hbm.shape
    width = depth // q
    main = cap // 16 * 16
    tail = cap - main
    own_h = win_ref.shape[0]
    n_main = experts * main
    me = lax.axis_index("expert")
    sec = lax.axis_index("section")
    near = experts // 2
    quarter = experts // 4
    half = me // near
    place = lax.rem(me, near)
    layer = me // quarter
    column = lax.rem(me, quarter)
    my_relay = lax.rem(layer + 2, 4) * quarter + column

    def cols(j):
        return pl.ds(pl.multiple_of(j * width, width), width)

    loads = [
        pltpu.make_async_copy(src, dst, loaded.at[i])
        for i, (src, dst) in enumerate(
            ((xf_hbm, xf_ref), (rf_hbm, rf_ref), (xb_hbm, xb_ref), (rb_hbm, rb_ref), (g_hbm, g_ref))
        )
    ]
    for load in loads:
        load.start()

    barrier = pltpu.get_barrier_semaphore()

    @pl.loop(1, experts)
    def _(k):
        pl.semaphore_signal(barrier, inc=1, device_id={"expert": lax.rem(me + k, experts)})

    @pl.loop(1, sections)
    def _(k):
        pl.semaphore_signal(barrier, inc=1, device_id={"section": lax.rem(sec + k, sections)})

    own_rows = pl.ds(pl.multiple_of(sec * own_h, own_h), own_h)
    for i, (src, dst) in enumerate(((win_ref, w_in), (wout_ref, w_out))):
        pltpu.make_async_copy(src, dst.at[own_rows], w_recv.at[i]).start()

    def routing(which, routes):
        lane_e = lax.broadcasted_iota(jnp.int32, (tokens, experts), 1)
        eye = (
            lax.broadcasted_iota(jnp.int32, (tokens, tokens), 0)
            == lax.broadcasted_iota(jnp.int32, (tokens, tokens), 1)
        ).astype(F32)
        columns = mm(eye.astype(BF16), routes.astype(F32).astype(BF16), NT)
        wide = [columns[:, k : k + 1] for k in range(routes.shape[0])]
        hits = [(i == lane_e.astype(F32)).astype(F32) for i in wide]
        table = functools.reduce(jnp.add, hits)
        later = (
            lax.broadcasted_iota(jnp.int32, (tokens, tokens), 0)
            > lax.broadcasted_iota(jnp.int32, (tokens, tokens), 1)
        ).astype(F32)
        rank = mm(later.astype(BF16), table.astype(BF16), NN)
        pos = [jnp.sum(h * rank, axis=1, keepdims=True) for h in hits]
        if main:
            lane = lax.broadcasted_iota(jnp.int32, (tokens, n_main), 1).astype(F32)
            hit = jnp.zeros((tokens, n_main), F32)
            for i, p in zip(wide, pos):
                hit = jnp.where(lane == jnp.where(p < main, i * main + p, -1.0), 1.0, hit)
            pm[which] = hit.astype(BF16)
        if tail:
            n_tail = experts * q * tail
            lane = lax.broadcasted_iota(jnp.int32, (tokens, n_tail), 1).astype(F32)
            for j in range(q):
                hit = jnp.zeros((tokens, n_tail), F32)
                for i, p in zip(wide, pos):
                    slot = jnp.where(p >= main, i * (q * tail) + (p - main) + j * tail, -1.0)
                    hit = jnp.where(lane == slot, 1.0, hit)
                pt[which, j] = hit.astype(BF16)

    def normalize(x_ref, which):
        @pl.loop(0, tokens // 16)
        def _(i):
            rows = pl.ds(pl.multiple_of(i * 16, 16), 16)
            x = x_ref[rows, :].astype(F32)
            inv = lax.rsqrt(jnp.mean(x * x, axis=-1, keepdims=True) + EPSILON)
            u_tok[which, rows, :] = (x * inv).astype(BF16)

    def dispatch(which, src, slot, group, side=half):
        chunks = pl.ds(group * near, near)
        if tail:
            tails[: near * q * tail, :] = jnp.zeros((near * q * tail, width), F32)

        @pl.loop(0, q)
        def _(j):
            piece = src[:, cols(j)]
            if main:
                lanes = pl.ds(pl.multiple_of(side * (near * main), near * main), near * main)
                send[slot, chunks, pl.ds(pl.multiple_of(j * main, main), main), :] = (
                    mm(pm[which, :, lanes], piece, TN).astype(BF16).reshape(near, main, width)
                )
            if tail:
                size = near * q * tail
                lanes = pl.ds(pl.multiple_of(side * size, size), size)
                tails[:size, :] += mm(pt[which, j, :, lanes], piece, TN)

        if tail:
            send[slot, chunks, q * main :, :] = (
                tails[: near * q * tail, :].astype(BF16).reshape(near, q * tail, width)
            )

    def to_near(slot, group, source, sem):
        pltpu.make_async_copy(
            send.at[slot, group * near + place], recv.at[slot, source], a2a_recv.at[slot]
        ).start()

        @pl.loop(1, near)
        def _(k):
            spot = lax.rem(place + k, near)
            pltpu.make_async_remote_copy(
                src_ref=send.at[slot, group * near + spot],
                dst_ref=recv.at[slot, source],
                send_sem=sem,
                recv_sem=a2a_recv.at[slot],
                device_id={"expert": half * near + spot},
            ).start()

    def to_far(slot):
        @pl.loop(0, near)
        def _(k):
            spot = lax.rem(place + k, near)
            pltpu.make_async_remote_copy(
                src_ref=send.at[slot, near + spot],
                dst_ref=recv.at[slot, me],
                send_sem=relay_send.at[slot],
                recv_sem=a2a_recv.at[slot],
                device_id={"expert": (1 - half) * near + spot},
            ).start()

    def to_relay(slot, src):
        pltpu.make_async_remote_copy(
            src_ref=src, dst_ref=far_tok.at[slot],
            send_sem=tok_send.at[slot], recv_sem=tok_recv.at[slot],
            device_id={"expert": my_relay},
        ).start()

    def routes_to_relay(micro, src):
        pltpu.make_async_remote_copy(
            src_ref=src, dst_ref=far_routes.at[micro],
            send_sem=route_send.at[micro], recv_sem=route_recv.at[micro],
            device_id={"expert": my_relay},
        ).start()

    def relay(slot):
        micro = min(slot, 1)

        if slot < 2:
            mine = far_routes.at[micro]
            pltpu.make_async_copy(mine, mine, route_recv.at[micro]).wait()
            routing(2, far_routes[micro])
        block = far_tok.at[slot]
        pltpu.make_async_copy(block, block, tok_recv.at[slot]).wait()
        dispatch(2, block, slot, 1)
        to_near(slot, 1, my_relay, relay_send.at[slot])

    def exchange(slot):
        pltpu.make_async_copy(home.at[slot - 3, me], recv.at[slot, me], a2a_recv.at[slot]).start()

        @pl.loop(1, experts)
        def _(k):
            peer = lax.rem(me + k, experts)
            pltpu.make_async_remote_copy(
                src_ref=home.at[slot - 3, peer],
                dst_ref=recv.at[slot, me],
                send_sem=a2a_send.at[slot],
                recv_sem=a2a_recv.at[slot],
                device_id={"expert": peer},
            ).start()

    def arrived(slot):
        pltpu.make_async_copy(recv.at[slot], recv.at[slot], a2a_recv.at[slot]).wait()

    def unpack(slot, rows_ref):
        buf = recv.at[slot]

        @pl.loop(0, q)
        def _(j):
            if main:
                rows_ref[:n_main, cols(j)] = buf[
                    :, pl.ds(pl.multiple_of(j * main, main), main), :
                ].reshape(n_main, width)
            if tail:
                for b in range(2):
                    packed = buf[b * near : (b + 1) * near, q * main :, :]
                    rows_ref[n_main + b * near * tail : n_main + (b + 1) * near * tail, cols(j)] = mm(
                        spread[j], packed.reshape(near * q * tail, width), NN
                    ).astype(BF16)

    def contract(rows_ref, weight, total):
        total[...] = jnp.zeros_like(total)

        @pl.loop(0, q)
        def _(j):
            total[...] += mm(rows_ref[:, cols(j)], weight[:, cols(j)], NT)

    def expand(weight, slot):
        buf = home.at[slot - 3]
        if tail:
            tails[...] = jnp.zeros_like(tails)

        @pl.loop(0, q)
        def _(j):
            out = mm(hid[...], weight[:, cols(j)], NN).astype(BF16)
            if main:
                buf[:, pl.ds(pl.multiple_of(j * main, main), main), :] = out[:n_main].reshape(
                    experts, main, width
                )
            if tail:
                for b in range(2):
                    block = out[n_main + b * near * tail : n_main + (b + 1) * near * tail]
                    packed = slice(b * near * q * tail, (b + 1) * near * q * tail)
                    tails[packed, :] += mm(spread[j], block, TN)

        if tail:
            buf[:, q * main :, :] = tails[...].astype(BF16).reshape(experts, q * tail, width)

    def combine(which, slot):
        buf = recv.at[slot]

        @pl.loop(0, q)
        def _(j):
            total = jnp.zeros((tokens, width), F32)
            if main:
                block = buf[:, pl.ds(pl.multiple_of(j * main, main), main), :]
                total += mm(pm[which], block.reshape(n_main, width), NN)
            if tail:
                packed = buf[:, q * main :, :].reshape(experts * q * tail, width)
                total += mm(pt[which, j], packed, NN)
            summed[:, cols(j)] = total

    def weight_terms(left, right, part):
        @pl.loop(0, q)
        def _(j):
            part[:, cols(j)] = mm(left, right[:, cols(j)], TN).astype(BF16)

    loads[0].wait()
    normalize(xf_ref, 0)
    loads[1].wait()
    loads[3].wait()
    pl.semaphore_wait(barrier, experts + sections - 2)
    to_relay(0, u_tok.at[0])
    routes_to_relay(0, rf_ref)
    routes_to_relay(1, rb_ref)
    routing(0, rf_ref[...])
    dispatch(0, u_tok.at[0], 0, 0)
    to_near(0, 0, me, a2a_send.at[0])
    for i, (src, dst) in enumerate(((win_ref, w_in), (wout_ref, w_out))):
        @pl.loop(1, sections)
        def _(k):
            pltpu.make_async_remote_copy(
                src_ref=src, dst_ref=dst.at[own_rows],
                send_sem=w_send.at[i], recv_sem=w_recv.at[i],
                device_id={"section": lax.rem(sec + k, sections)},
            ).start()

    loads[2].wait()
    normalize(xb_ref, 1)
    loads[4].wait()
    to_relay(1, u_tok.at[1])
    routing(1, rb_ref[...])
    dispatch(1, u_tok.at[1], 1, 0)
    to_near(1, 0, me, a2a_send.at[1])
    dispatch(1, g_ref, 2, 1, 1 - half)
    to_far(2)
    dispatch(1, g_ref, 2, 0)
    to_near(2, 0, me, a2a_send.at[2])

    if tail:
        shape = (near * tail, near * q * tail)
        row = lax.broadcasted_iota(jnp.int32, shape, 0).astype(F32)
        col = lax.broadcasted_iota(jnp.int32, shape, 1).astype(F32)
        start = row + jnp.floor((row + 0.5) * (1.0 / tail)) * ((q - 1) * tail)
        for j in range(q):
            spread[j] = jnp.where(col == start + j * tail, 1.0, 0.0).astype(BF16)

    for i, dst in enumerate((w_in, w_out)):
        pltpu.make_async_copy(dst, dst, w_recv.at[i]).wait()

    relay(0)
    arrived(0)
    unpack(0, u_rows)
    contract(u_rows, w_in, act)
    hid[...] = jax.nn.silu(act[...]).astype(BF16)
    expand(w_out, 3)
    exchange(3)

    relay(1)
    arrived(1)
    unpack(1, u_rows)
    contract(u_rows, w_in, act)
    arrived(2)
    unpack(2, g_rows)
    contract(g_rows, w_out, slope)
    sigma = jax.nn.sigmoid(act[...])
    hid[...] = (slope[...] * (sigma * (1.0 + act[...] * (1.0 - sigma)))).astype(BF16)
    expand(w_in, 4)
    exchange(4)
    weight_terms(hid[...], u_rows, part_in)
    hid[...] = jax.nn.silu(act[...]).astype(BF16)
    weight_terms(hid[...], g_rows, part_out)
    for i, (part, out) in enumerate(((part_in, gin_ref), (part_out, gout_ref))):
        pltpu.make_async_copy(part.at[own_rows], out.at[sec], p_recv.at[i]).start()

        @pl.loop(1, sections)
        def _(k):
            peer = lax.rem(sec + k, sections)
            pltpu.make_async_remote_copy(
                src_ref=part.at[pl.ds(pl.multiple_of(peer * own_h, own_h), own_h)],
                dst_ref=out.at[sec],
                send_sem=p_send.at[i], recv_sem=p_recv.at[i],
                device_id={"section": peer},
            ).start()

    arrived(3)
    combine(0, 3)

    @pl.loop(0, tokens // 16)
    def _(i):
        rows = pl.ds(pl.multiple_of(i * 16, 16), 16)
        result[0, rows, :] = (xf_ref[rows, :].astype(F32) + summed[rows, :]).astype(BF16)

    to_next = pltpu.make_async_remote_copy(
        src_ref=result.at[0], dst_ref=next_ref, send_sem=s_send.at[0], recv_sem=s_recv.at[0],
        device_id={"section": lax.rem(sec + 1, sections)},
    )
    to_next.start()

    arrived(4)
    combine(1, 4)

    @pl.loop(0, tokens // 16)
    def _(i):
        rows = pl.ds(pl.multiple_of(i * 16, 16), 16)
        x = xb_ref[rows, :].astype(F32)
        total = summed[rows, :]
        inv = lax.rsqrt(jnp.mean(x * x, axis=-1, keepdims=True) + EPSILON)
        proj = jnp.mean(total * x, axis=-1, keepdims=True)
        grad = g_ref[rows, :].astype(F32) + inv * total - x * (inv * inv * inv) * proj
        result[1, rows, :] = grad.astype(BF16)

    to_prev = pltpu.make_async_remote_copy(
        src_ref=result.at[1], dst_ref=prev_ref, send_sem=s_send.at[1], recv_sem=s_recv.at[1],
        device_id={"section": lax.rem(sec + sections - 1, sections)},
    )
    to_prev.start()

    for i, (src, out) in enumerate(((win_ref, gin_ref), (wout_ref, gout_ref))):
        pltpu.make_async_copy(out, out, p_recv.at[i]).wait()

        @pl.loop(1, sections)
        def _(k):
            pltpu.make_async_copy(src, src, w_send.at[i]).wait()
            pltpu.make_async_copy(src, src, p_send.at[i]).wait()

    fewer = send.at[0, pl.ds(0, near - 1)]
    for slot in range(3):
        pltpu.make_async_copy(fewer, fewer, a2a_send.at[slot]).wait()
        if slot < 2:
            pltpu.make_async_copy(g_ref, g_ref, tok_send.at[slot]).wait()
        relayed = send.at[0, pl.ds(0, near if slot == 2 else near - 1)]
        pltpu.make_async_copy(relayed, relayed, relay_send.at[slot]).wait()

    for micro, src in enumerate((rf_ref, rb_ref)):
        pltpu.make_async_copy(src, src, route_send.at[micro]).wait()
    others = home.at[0, pl.ds(0, experts - 1)]
    for slot in (3, 4):
        pltpu.make_async_copy(others, others, a2a_send.at[slot]).wait()
    to_next.wait()
    to_prev.wait()


def per_device(fwd_states, fwd_routes, bwd_states, bwd_routes, bwd_cot, w_in, w_out):
    experts, sections = lax.axis_size("expert"), lax.axis_size("section")
    _, tokens, depth = fwd_states.shape
    top = fwd_routes.shape[2]
    own_h = w_in.shape[1]
    full_h = own_h * sections
    q = GROUPS
    cap = max(2, (5 * tokens * top + 4 * experts - 1) // (4 * experts))
    cap = -(-cap // 4) * 4
    main = cap // 16 * 16
    tail = cap - main
    rows = experts * cap
    width = depth // q
    n_tail = max(16, experts * q * tail)
    grant = (46 if experts * cap <= 512 and full_h * experts <= 8192 else 62) * 1000 * 1024
    anywhere = pl.BlockSpec(memory_space=pl.ANY)
    sems = pltpu.SemaphoreType.DMA
    states = jax.ShapeDtypeStruct((tokens, depth), BF16)
    parts = jax.ShapeDtypeStruct((sections, own_h, depth), BF16)
    next_states, prev_cot, part_in, part_out = pl.pallas_call(
        functools.partial(kernel, experts, sections, cap),
        out_shape=(states, states, parts, parts),
        in_specs=[pl.BlockSpec(memory_space=pltpu.HBM)] * 7,
        out_specs=(anywhere,) * 4,
        scratch_shapes=[
            pltpu.VMEM((tokens, depth), BF16),
            pltpu.VMEM((top, tokens), jnp.int32),
            pltpu.VMEM((tokens, depth), BF16),
            pltpu.VMEM((top, tokens), jnp.int32),
            pltpu.VMEM((tokens, depth), BF16),
            pltpu.VMEM((3, experts, q * cap, width), BF16),
            pltpu.VMEM((2, experts, q * cap, width), BF16),
            pltpu.VMEM((5, experts, q * cap, width), BF16),
            pltpu.VMEM((full_h, depth), BF16),
            pltpu.VMEM((full_h, depth), BF16),
            pltpu.VMEM((2, tokens, depth), BF16),
            pltpu.VMEM((3, tokens, depth), BF16),
            pltpu.VMEM((2, top, tokens), jnp.int32),
            pltpu.VMEM((rows, depth), BF16),
            pltpu.VMEM((rows, depth), BF16),
            pltpu.VMEM((rows, full_h), F32),
            pltpu.VMEM((rows, full_h), F32),
            pltpu.VMEM((rows, full_h), BF16),
            pltpu.VMEM((n_tail, width), F32),
            pltpu.VMEM((full_h, depth), BF16),
            pltpu.VMEM((full_h, depth), BF16),
            pltpu.VMEM((3, tokens, max(16, experts * main)), BF16),
            pltpu.VMEM((3, q, tokens, n_tail), BF16),
            pltpu.VMEM((q, max(16, experts // 2 * tail), max(16, experts // 2 * q * tail)), BF16),
            pltpu.VMEM((tokens, depth), F32),
            pltpu.VMEM((2, tokens, depth), BF16),
            sems((5,)), sems((5,)), sems((5,)), sems((3,)), sems((3,)), sems((2,)), sems((2,)), sems((3,)),
            sems((2,)), sems((2,)),
            sems((2,)), sems((2,)), sems((2,)), sems((2,)),
        ],
        compiler_params=pltpu.CompilerParams(
            collective_id=0, has_side_effects=True, vmem_limit_bytes=grant
        ),
    )(fwd_states[0], fwd_routes[0].T, bwd_states[0], bwd_routes[0].T, bwd_cot[0], w_in[0], w_out[0])
    grad_in = jnp.sum(part_in.astype(F32), axis=0)
    grad_out = jnp.sum(part_out.astype(F32), axis=0)
    return next_states[None], prev_cot[None], grad_in[None], grad_out[None]


def solution(mesh):
    in_specs = (P("section", "expert", None),) * 5 + (P("expert", "section", None),) * 2
    out_specs = (P("section", "expert", None),) * 2 + (P("expert", "section", None),) * 2
    return jax.shard_map(
        per_device, mesh=mesh, in_specs=in_specs, out_specs=out_specs, check_vma=False
    )
```
